32 devices in a mesh: parts: 2 (over x), view: 8 (over z, y), slab: 2 (over core).
Axes of the slice: x: 2, y: 2, z: 4, core: 2. Of those that a mesh axis runs over, the one named last changes fastest.
Arguments:
- activity: bfloat16 [128, 32, 256], P(('parts', 'view'), 'slab'), parts along dimension 0, may hold values from 0.6 to 11.2
- histo_counts: int32 [32, 64, 32, 256], P(('parts', 'view'), None, 'slab'), parts along dimension 0, may hold values from 0 to 22
- background: bfloat16 [32, 32, 256], P(('parts', 'view'), 'slab'), parts along dimension 0, may hold values from 0.5 to 2
- blur_values: bfloat16 [16, 3, 256, 32], P('view'), may hold values from 0.0041503906 to 0.020751953
- band_start: int32 [16, 3, 256], P('view'), may hold values from 0 to 224, as said below
Outputs:
- gradient: float32 [128, 32, 256], P(('parts', 'view'), 'slab'), parts along dimension 0
The draws below stay inside these ranges and needn't reach their ends.
There are 2 independent parts, one for each index of `parts`. The reference program is written for one: setup_inputs(seed, part) draws one part's arguments, and reference() takes and returns one part's arrays. A program takes and returns all parts, laid end to end along the dimension named above; an argument that names none is the same for every part. Nothing has to cross between parts.
Inputs may be any that keep to these rules, and one draw needn't show every extreme that they name: Each band lies inside the matrix: columns band_start to band_start + 31.
All inputs are finite; a program needn't handle non-finite values.
Results may differ from the reference program's by a relative error of at most 0.0003.
Values may be sent and summed in bfloat16 or wider, within the bound.
A program may use at most 64 MiB of HBM per device.

```python
import math
import jax
import jax.numpy as jnp
from jax import lax

NX = 256
BAND = 32
TAPS = 3
NY = 64
NZ = 32
VIEWS = 16


def level_grid(key):
    keyed = jax.random.fold_in(key, 11)
    levels = jax.random.randint(keyed, (NY, NZ), 0, 7)
    return levels.at[0, 0].set(6).astype(jnp.int32)


def draw_activity(key, part):
    levels = level_grid(key)
    scales = jnp.exp2(levels.astype(jnp.float32) * 0.5)
    uniform_part = jax.random.uniform(jax.random.fold_in(key, 13), (NY, NZ, NX), jnp.float32)
    factor = 0.6 + 0.8 * uniform_part
    return (scales[:, :, None] * factor).astype(jnp.bfloat16)


def draw_histo_counts(key, part):
    levels = level_grid(key)
    table = jnp.array([2, 3, 4, 5, 6, 8, 11], jnp.int32)
    means = table[levels]
    upper = 2 * means[None, :, :, None] + 1
    counts = jax.random.randint(jax.random.fold_in(key, 17), (VIEWS, NY, NZ, NX), 0, upper)
    counts = counts.at[0, 0, 0, 0].set(22)
    counts = counts.at[0, 0, 0, 1].set(0)
    return counts.astype(jnp.int32)


def draw_band_start(key, part):
    keyed = jax.random.fold_in(key, 7)
    first_key, second_key = jax.random.split(keyed)
    reach = max(BAND // 4, 1)
    offsets = jax.random.randint(first_key, (VIEWS, TAPS, 1), -reach, reach + 1)
    jitters = jax.random.randint(second_key, (VIEWS, TAPS, NX), -1, 2)
    positions = jnp.arange(NX, dtype=jnp.int32)[None, None, :]
    return jnp.clip(positions - BAND // 2 + offsets + jitters, 0, NX - BAND).astype(jnp.int32)


def level_of(rng, dims, shards, smallest, largest):
    level = 1.0
    for axis_at, shards_of in shards:
        heights = jax.random.uniform(jax.random.fold_in(jax.random.fold_in(rng, 6), axis_at), (shards_of,), jnp.float32, smallest / len(shards), largest / len(shards))
        level = level * jnp.repeat(jnp.exp(heights), dims[axis_at] // shards_of).reshape((-1,) + (1,) * (len(dims) - 1 - axis_at))
    return level


def setup_inputs(seed: int = 0, part: int = 0) -> dict:
    seeds = jax.random.split(jax.random.key(seed), 6)
    part_keys = jax.random.split(jax.random.fold_in(seeds[5], part), 6)
    return {
        "activity": draw_activity(jax.random.fold_in(jax.random.fold_in(seeds[5], part), 71), part),
        "histo_counts": draw_histo_counts(jax.random.fold_in(jax.random.fold_in(seeds[5], part), 71), part),
        "background": jnp.clip(jnp.exp(math.log(2.0) - 1.3862944 * jax.random.uniform(part_keys[2], (VIEWS, NZ, NX), jnp.float32) ** level_of(part_keys[2], (VIEWS, NZ, NX), ((0, 8), (1, 2)), -0.2, 0.2)), 0.5, 2.0).astype(jnp.bfloat16),
        "blur_values": jnp.clip(0.0041503906 + 0.016601562 * jax.random.uniform(seeds[3], (VIEWS, TAPS, NX, BAND), jnp.float32) ** level_of(seeds[3], (VIEWS, TAPS, NX, BAND), ((0, 8),), -0.2, 0.2), 0.0041503906, 0.020751953).astype(jnp.bfloat16),
        "band_start": draw_band_start(jax.random.fold_in(seeds[5], 71), part),
    }


def blur_matrix(band_values, band_starts):
    width_x = band_values.shape[0]
    band_width = band_values.shape[1]
    columns = jnp.arange(width_x, dtype=jnp.int32)
    distance = columns[None, :] - band_starts.astype(jnp.int32)[:, None]
    selector = (distance[:, :, None] == jnp.arange(band_width, dtype=jnp.int32)[None, None, :]).astype(jnp.float32)
    return jnp.einsum('ik,ijk->ij', band_values.astype(jnp.float32), selector).astype(jnp.bfloat16)


def view_gradient(activity, view_counts, view_background, view_values, view_starts):
    rows_y, slices, width_x = activity.shape
    matrices = [blur_matrix(view_values[tap_index], view_starts[tap_index]) for tap_index in range(3)]
    padded = jnp.pad(activity, ((0, 0), (1, 1), (0, 0)))
    summed = jnp.zeros((rows_y * slices, width_x), jnp.float32)
    for tap_index in range(3):
        shifted = padded[:, tap_index:tap_index + slices, :].reshape(-1, width_x)
        summed = summed + jnp.dot(shifted, matrices[tap_index].T, preferred_element_type=jnp.float32)
    expected = summed.reshape(rows_y, slices, width_x) + view_background.astype(jnp.float32)[None]
    ratio_bf = (view_counts.astype(jnp.float32) / expected - 1.0).astype(jnp.bfloat16)
    widened = jnp.pad(ratio_bf, ((0, 0), (1, 1), (0, 0)))
    back_sum = jnp.zeros((rows_y * slices, width_x), jnp.float32)
    for tap_index in range(3):
        shifted = widened[:, 2 - tap_index:2 - tap_index + slices, :].reshape(-1, width_x)
        back_sum = back_sum + jnp.dot(shifted, matrices[tap_index], preferred_element_type=jnp.float32)
    return back_sum.reshape(rows_y, slices, width_x)


def reference(activity, histo_counts, background, blur_values, band_start):
    def one_view(carry, inputs):
        view_counts, view_background, view_values, view_starts = inputs
        return carry + view_gradient(activity, view_counts, view_background, view_values, view_starts), None

    start_value = jnp.zeros(activity.shape, jnp.float32)
    gradient, _ = lax.scan(one_view, start_value, (histo_counts, background, blur_values, band_start))
    return gradient
```

```python
import functools

import jax
import jax.numpy as jnp
from jax import lax
from jax.experimental import pallas as pl
from jax.experimental.pallas import tpu as pltpu
from jax.sharding import PartitionSpec as P

MESH = pl.DeviceIdType.MESH
PAIR = 2


CODE_MAX = 32767.0
TINY = 1e-30
VMEM_LIMIT = 63 << 20


def encode(block):
    top = jnp.max(jnp.abs(block), axis=(0, 1), keepdims=False)[None, :]
    scale = jnp.where(top > TINY, CODE_MAX / jnp.maximum(top, TINY), 0.0)
    code = jnp.round(block * scale[None]).astype(jnp.int32).astype(jnp.int16)
    return code, top * (1.0 / CODE_MAX)


def decode(code, unit):
    return code.astype(jnp.int32).astype(jnp.float32) * unit[None]


def kernel(
    groups, rows, act_hbm, counts_hbm, back_hbm, values_hbm, starts_hbm, out_ref,
    back_ref, values_ref, starts_ref,
    acts, edge_own, counts, forward_w, backward_w, whole, kept, part_code, part_unit, pair_code, pair_unit,
    sum_code, sum_unit, owner_code, owner_unit, halo_out, halo_in,
    load_sem, counts_sem, ready, pair_ready, line_send, line_recv, line_edge_send, line_edge_recv,
    pair_send, pair_recv, pair_edge_send, pair_edge_recv, edge_send, edge_recv, halo_send, halo_recv,
    part_send, part_recv, part_unit_send, part_unit_recv, sum_send, sum_recv, sum_unit_send, sum_unit_recv,
):
    part = lax.axis_index("parts")
    view = lax.axis_index("view")
    slab = lax.axis_index("slab")
    last = groups - 1
    hi = view // PAIR
    lo = view % PAIR
    other = 1 - lo
    area, width = act_hbm.shape
    slices = area // rows
    views = back_ref.shape[0]
    taps = values_ref.shape[0] // views
    group_rows = PAIR * rows

    def at(hi_index, lo_index, slab_index):
        return (part, hi_index * PAIR + lo_index, slab_index)

    def near(step):
        both = jnp.minimum(hi, last - hi)
        reach = (step + 1) // 2
        around = jnp.where(step % 2 == 1, hi - reach, hi + reach)
        beyond = jnp.where(hi < last - hi, step, last - step)
        return jnp.where(step <= 2 * both, around, beyond)

    barrier = pltpu.get_barrier_semaphore()
    pl.semaphore_signal(barrier, inc=1, device_id=at(hi, lo, 1 - slab), device_id_type=MESH)

    @pl.when(lo == 0)
    def _():
        pl.semaphore_signal(barrier, inc=1, device_id=at(hi, 1, slab), device_id_type=MESH)

    for index in range(1, groups):

        @pl.when(index > hi)
        def _():
            pl.semaphore_signal(barrier, inc=1, device_id=at(index, lo, slab), device_id_type=MESH)

    def counts_copy(step):
        first = pl.multiple_of(near(step) * group_rows, group_rows)
        return pltpu.make_async_copy(
            counts_hbm.at[:, pl.ds(first, group_rows)], counts.at[step], counts_sem.at[step]
        )

    def block_of(index):
        return acts.at[index, pl.ds(0, area)]

    def edge_of(index):
        return acts.at[index, pl.ds(area, rows)]

    loads = [
        pltpu.make_async_copy(source, target, load_sem.at[index])
        for index, (source, target) in enumerate(
            (
                (act_hbm, block_of(view)), (values_hbm, values_ref), (starts_hbm, starts_ref),
                (back_hbm, back_ref),
            )
        )
    ]
    for load in loads:
        load.start()
    for step in range(groups):
        counts_copy(step).start()
    loads[0].wait()
    own = acts[view, :area].astype(jnp.float32).reshape(rows, slices, width)
    edge_own[...] = jnp.where(slab == 0, own[:, slices - 1, :], own[:, 0, :]).astype(jnp.bfloat16)

    def line_copy(index):
        return pltpu.make_async_remote_copy(
            src_ref=act_hbm, dst_ref=block_of(view),
            send_sem=line_send.at[index], recv_sem=line_recv.at[hi],
            device_id=at(index, lo, slab), device_id_type=MESH,
        )

    def line_edge_copy(index):
        return pltpu.make_async_remote_copy(
            src_ref=edge_of(view), dst_ref=edge_of(view),
            send_sem=line_edge_send.at[index], recv_sem=line_edge_recv.at[hi],
            device_id=at(index, lo, slab), device_id_type=MESH,
        )

    def line_wait(index):
        source = index * PAIR + lo
        for target, recv in ((block_of(source), line_recv), (edge_of(source), line_edge_recv)):
            pltpu.make_async_remote_copy(
                src_ref=target, dst_ref=target,
                send_sem=line_send.at[index], recv_sem=recv.at[index],
                device_id=at(hi, other, slab), device_id_type=MESH,
            ).wait_recv()

    def pair_copy(index, source):
        return pltpu.make_async_remote_copy(
            src_ref=source, dst_ref=block_of(index * PAIR + lo),
            send_sem=pair_send.at[index], recv_sem=pair_recv.at[index],
            device_id=at(hi, other, slab), device_id_type=MESH,
        )

    def pair_edge_copy(index):
        return pltpu.make_async_remote_copy(
            src_ref=edge_of(index * PAIR + lo), dst_ref=edge_of(index * PAIR + lo),
            send_sem=pair_edge_send.at[index], recv_sem=pair_edge_recv.at[index],
            device_id=at(hi, other, slab), device_id_type=MESH,
        )

    edge_copy = pltpu.make_async_remote_copy(
        src_ref=edge_own, dst_ref=edge_of(view), send_sem=edge_send, recv_sem=edge_recv,
        device_id=at(hi, lo, 1 - slab), device_id_type=MESH,
    )

    pl.semaphore_wait(barrier, 1 + hi + lo)

    @pl.when(lo == 1)
    def _():
        pl.semaphore_signal(pair_ready, inc=1, device_id=at(hi, 0, slab), device_id_type=MESH)

    for index in range(last):

        @pl.when(index < hi)
        def _():
            pl.semaphore_signal(ready.at[hi], inc=1, device_id=at(index, lo, slab), device_id_type=MESH)

    edge_copy.start()
    for index in range(last):

        @pl.when(index < hi)
        def _():
            line_copy(index).start()

    @pl.when(lo == 0)
    def _():
        pl.semaphore_wait(pair_ready, 1)

    pair_copy(hi, act_hbm).start()

    @pl.when(hi < last)
    def _():
        pl.semaphore_wait(ready.at[hi + 1], 1)
        line_copy(hi + 1).start()

    for load in loads[1:]:
        load.wait()

    def build(which):
        view_index, tap = which // taps, which % taps
        start = starts_ref[tap, view_index : view_index + 1, :]
        turned = jnp.concatenate(
            [values_ref[which].astype(jnp.float32), jnp.zeros((8, width), jnp.float32)], axis=0
        )
        shift = 1
        while shift < 8:
            turned = jnp.where((start & shift) != 0, pltpu.roll(turned, shift, axis=0), turned)
            shift *= 2
        while shift < width:
            extra = min(shift, width - turned.shape[0])
            plain = jnp.concatenate([turned, jnp.zeros((extra, width), jnp.float32)], axis=0)
            moved = jnp.concatenate([jnp.zeros((shift, width), jnp.float32), turned], axis=0)[: plain.shape[0]]
            turned = jnp.where((start & shift) != 0, moved, plain)
            shift *= 2
        forward_w[tap * width : (tap + 1) * width, view_index * width : (view_index + 1) * width] = (
            turned.astype(jnp.bfloat16)
        )
        backward_w[view_index * width : (view_index + 1) * width, tap * width : (tap + 1) * width] = (
            turned.T.astype(jnp.bfloat16)
        )

    total = views * taps
    for which in range(total // 2):
        build(which)

    edge_copy.wait_recv()
    for index in range(last):

        @pl.when(index < hi)
        def _():
            line_edge_copy(index).start()

    pair_edge_copy(hi).start()

    @pl.when(hi < last)
    def _():
        line_edge_copy(hi + 1).start()

    for which in range(total // 2, total):
        build(which)

    for index in range(2, groups):

        @pl.when(index > hi + 1)
        def _():
            pl.semaphore_wait(ready.at[index], 1)
            line_copy(index).start()
            line_edge_copy(index).start()

    slice_at = lax.broadcasted_iota(jnp.int32, (group_rows, slices, width), 1)
    inner = jnp.where(slab == 0, slices - 1, 0)

    def halo_copy(step):
        return pltpu.make_async_remote_copy(
            src_ref=halo_out.at[step], dst_ref=halo_in.at[step],
            send_sem=halo_send.at[step], recv_sem=halo_recv.at[step],
            device_id=at(hi, lo, 1 - slab), device_id_type=MESH,
        )

    def part_copies(step):
        return [
            pltpu.make_async_remote_copy(
                src_ref=source.at[step], dst_ref=landing.at[step],
                send_sem=send.at[step], recv_sem=recv.at[step],
                device_id=at(hi, other, slab), device_id_type=MESH,
            )
            for source, landing, send, recv in (
                (part_unit, pair_unit, part_unit_send, part_unit_recv),
                (part_code, pair_code, part_send, part_recv),
            )
        ]

    def sum_copies(step, landing_at):
        return [
            pltpu.make_async_remote_copy(
                src_ref=source.at[step], dst_ref=landing.at[landing_at],
                send_sem=send.at[step], recv_sem=recv.at[landing_at],
                device_id=at(near(step), lo, slab), device_id_type=MESH,
            )
            for source, landing, send, recv in (
                (sum_unit, owner_unit, sum_unit_send, sum_unit_recv),
                (sum_code, owner_code, sum_send, sum_recv),
            )
        ]

    def relay(step):
        index = near(step)
        line_wait(index)
        pair_copy(index, block_of(index * PAIR + lo)).start()
        pair_edge_copy(index).start()

    def joined(step):
        for copy in part_copies(step):
            copy.wait_recv()
        return kept[step] + decode(pair_code[step], pair_unit[step])

    def pass_on(step):
        sum_code[step], sum_unit[step] = encode(joined(step))
        for copy in sum_copies(step, hi):
            copy.start()

    def one_group(step, carry):
        group = near(step)

        @pl.when(step < last)
        def _():
            relay(step + 1)

        pair_copy(group, block_of(group * PAIR + lo)).wait_recv()
        pair_edge_copy(group).wait_recv()
        blocks = acts[pl.ds(group * PAIR, PAIR)].astype(jnp.float32)
        image = blocks[:, :area].reshape(group_rows, slices, width)
        edge = blocks[:, area : area + rows].reshape(group_rows, 1, width)
        lower = jnp.where(slice_at == 0, jnp.where(slab == 0, 0.0, edge), pltpu.roll(image, 1, axis=1))
        upper = jnp.where(
            slice_at == slices - 1, jnp.where(slab == 0, edge, 0.0), pltpu.roll(image, slices - 1, axis=1)
        )
        stacked = jnp.concatenate(
            [x.reshape(-1, width).astype(jnp.bfloat16) for x in (lower, image, upper)], axis=1
        )
        summed = jnp.dot(stacked, forward_w[...], preferred_element_type=jnp.float32)
        counts_copy(step).wait()
        ratios = []
        ratio_edges = []
        for view_index in range(views):
            expected = (
                summed[:, view_index * width : (view_index + 1) * width].reshape(group_rows, slices, width)
                + back_ref[view_index].astype(jnp.float32)[None]
            )
            ratio = counts[step, view_index].astype(jnp.float32) / expected - 1.0
            ratio_edges.append(
                jnp.where(slab == 0, ratio[:, slices - 1, :], ratio[:, 0, :]).astype(jnp.bfloat16)
            )
            ratios.append(ratio.reshape(-1, width).astype(jnp.bfloat16))
        outer = pl.multiple_of((1 - slab) * ((taps - 1) * width), width)
        halo_out[step] = jnp.dot(
            jnp.concatenate(ratio_edges, axis=1), backward_w[:, pl.ds(outer, width)],
            preferred_element_type=jnp.float32,
        ).reshape(PAIR, rows, width)
        halo_copy(step).start()
        spread = jnp.dot(
            jnp.concatenate(ratios, axis=1), backward_w[...], preferred_element_type=jnp.float32
        ).reshape(group_rows, slices, taps * width)
        from_upper = pltpu.roll(spread[:, :, :width], slices - 1, axis=1)
        from_lower = pltpu.roll(spread[:, :, 2 * width :], 1, axis=1)
        from_upper = jnp.where(slice_at == slices - 1, 0.0, from_upper)
        from_lower = jnp.where(slice_at == 0, 0.0, from_lower)
        whole[...] = (spread[:, :, width : 2 * width] + from_upper + from_lower).reshape(
            PAIR, rows, slices, width
        )
        halo_copy(step).wait_recv()

        def with_halo(which):
            return whole[which] + jnp.where(
                slice_at[:rows] == inner, halo_in[step, which].reshape(rows, 1, width), 0.0
            )

        part_code[step], part_unit[step] = encode(with_halo(other))
        for copy in part_copies(step):
            copy.start()
        kept[step] = with_halo(lo)

        @pl.when(step > 1)
        def _():
            pass_on(step - 1)

        return carry

    lax.fori_loop(0, groups, one_group, 0)
    pass_on(last)
    out_ref[...] = joined(0)
    for step in range(1, groups):
        for copy in sum_copies(step, near(step)):
            copy.wait_recv()
        out_ref[...] += decode(owner_code[near(step)], owner_unit[near(step)])

    for index in range(groups):

        @pl.when(index != hi)
        def _():
            line_copy(index).wait_send()
            line_edge_copy(index).wait_send()

        pair_copy(index, act_hbm).wait_send()
        pair_edge_copy(index).wait_send()
    edge_copy.wait_send()
    for step in range(groups):
        halo_copy(step).wait_send()
        for copy in part_copies(step):
            copy.wait_send()
    for step in range(1, groups):
        for copy in sum_copies(step, hi):
            copy.wait_send()


def per_device(activity, histo_counts, background, blur_values, band_start):
    members = lax.axis_size("view")
    groups = members // PAIR
    rows, slices, width = activity.shape
    views, taps, _, band = blur_values.shape
    group_rows = PAIR * rows
    area = rows * slices
    dma = pltpu.SemaphoreType.DMA
    block = (rows, slices, width)
    vmem = pl.BlockSpec(memory_space=pltpu.VMEM)
    unit = (groups, 1, width)
    return pl.pallas_call(
        functools.partial(kernel, groups, rows),
        out_shape=jax.ShapeDtypeStruct(block, jnp.float32),
        in_specs=[pl.BlockSpec(memory_space=pl.ANY)] * 5,
        out_specs=vmem,
        scratch_shapes=[
            pltpu.VMEM(background.shape, jnp.bfloat16),
            pltpu.VMEM((views * taps, band, width), jnp.bfloat16),
            pltpu.VMEM((taps, views, width), jnp.int32),
            pltpu.VMEM((members, area + rows, width), jnp.bfloat16),
            pltpu.VMEM((rows, width), jnp.bfloat16),
            pltpu.VMEM((groups, views, group_rows, slices, width), jnp.int32),
            pltpu.VMEM((taps * width, views * width), jnp.bfloat16),
            pltpu.VMEM((views * width, taps * width), jnp.bfloat16),
            pltpu.VMEM((PAIR,) + block, jnp.float32),
            pltpu.VMEM((groups,) + block, jnp.float32),
            pltpu.VMEM((groups,) + block, jnp.int16),
            pltpu.VMEM(unit, jnp.float32),
            pltpu.VMEM((groups,) + block, jnp.int16),
            pltpu.VMEM(unit, jnp.float32),
            pltpu.VMEM((groups,) + block, jnp.int16),
            pltpu.VMEM(unit, jnp.float32),
            pltpu.VMEM((groups,) + block, jnp.int16),
            pltpu.VMEM(unit, jnp.float32),
            pltpu.VMEM((groups, PAIR, rows, width), jnp.float32),
            pltpu.VMEM((groups, PAIR, rows, width), jnp.float32),
            dma((4,)),
            dma((groups,)),
            pltpu.SemaphoreType.REGULAR((groups,)),
            pltpu.SemaphoreType.REGULAR,
            dma((groups,)), dma((groups,)), dma((groups,)), dma((groups,)),
            dma((groups,)), dma((groups,)), dma((groups,)), dma((groups,)),
            dma, dma,
            dma((groups,)), dma((groups,)),
            dma((groups,)), dma((groups,)), dma((groups,)), dma((groups,)),
            dma((groups,)), dma((groups,)), dma((groups,)), dma((groups,)),
        ],
        compiler_params=pltpu.CompilerParams(collective_id=0, has_side_effects=True, vmem_limit_bytes=VMEM_LIMIT),
        name="poisson_gradient",
    )(
        activity.reshape(area, width), histo_counts, background,
        jnp.swapaxes(blur_values, 2, 3).reshape(views * taps, band, width), jnp.swapaxes(band_start, 0, 1),
    )


def solution(mesh):
    placed = (
        P(("parts", "view"), "slab", None),
        P(("parts", "view"), None, "slab", None),
        P(("parts", "view"), "slab", None),
        P("view", None, None, None),
        P("view", None, None),
    )
    return jax.shard_map(
        per_device,
        mesh=mesh,
        in_specs=placed,
        out_specs=P(("parts", "view"), "slab", None),
        check_vma=False,
    )
```

```python
import functools

import jax
import jax.numpy as jnp
from jax import lax
from jax.experimental import pallas as pl
from jax.experimental.pallas import tpu as pltpu
from jax.sharding import PartitionSpec as P

MESH = pl.DeviceIdType.MESH
PAIR = 2


CODE_MAX = 32767.0
TINY = 1e-30
VMEM_LIMIT = 63 << 20


def encode(block):
    top = jnp.max(jnp.abs(block), axis=(0, 1), keepdims=False)[None, :]
    scale = jnp.where(top > TINY, CODE_MAX / jnp.maximum(top, TINY), 0.0)
    code = jnp.round(block * scale[None]).astype(jnp.int32).astype(jnp.int16)
    return code, top * (1.0 / CODE_MAX)


def decode(code, unit):
    return code.astype(jnp.int32).astype(jnp.float32) * unit[None]


def kernel(
    groups, act_hbm, counts_hbm, back_hbm, values_hbm, starts_hbm, out_ref,
    back_ref, values_ref, starts_ref,
    acts, edge_own, counts, counts_raw, counts_out, counts_in, forward_w, backward_w, whole,
    sum_code, sum_unit, owner_code, owner_unit, halo_out, halo_in,
    load_sem, counts_sem, raw_sem, ready, pair_ready, line_send, line_recv, line_edge_send, line_edge_recv,
    swap_send, swap_recv, share_send, share_recv, trade_send, trade_recv,
    edge_send, edge_recv, halo_send, halo_recv, sum_send, sum_recv, sum_unit_send, sum_unit_recv,
):
    part = lax.axis_index("parts")
    view = lax.axis_index("view")
    slab = lax.axis_index("slab")
    last = groups - 1
    hi = view // PAIR
    lo = view % PAIR
    other = 1 - lo
    rows, slices, width = out_ref.shape
    area = rows * slices
    views = back_hbm.shape[0]
    total = values_hbm.shape[0]
    taps = total // views
    half = total // 2

    def at(hi_index, lo_index, slab_index):
        return (part, hi_index * PAIR + lo_index, slab_index)

    def cross(first, second):
        index, unit = 0, 1
        while unit < groups:
            index += ((first // unit + second // unit) % 2) * unit
            unit *= 2
        return index

    def met(step):
        return cross(hi, (groups - step) % groups)

    def step_of(index):
        return (groups - cross(hi, index)) % groups

    barrier = pltpu.get_barrier_semaphore()
    pl.semaphore_signal(barrier, inc=1, device_id=at(hi, lo, 1 - slab), device_id_type=MESH)

    @pl.when(lo == 0)
    def _():
        pl.semaphore_signal(barrier, inc=1, device_id=at(hi, 1, slab), device_id_type=MESH)

    for index in range(1, groups):

        @pl.when(index > hi)
        def _():
            pl.semaphore_signal(barrier, inc=1, device_id=at(index, lo, slab), device_id_type=MESH)

    def counts_copy(step, column, target, sems):
        first = pl.multiple_of((met(step) * PAIR + column) * rows, rows)
        return pltpu.make_async_copy(counts_hbm.at[:, pl.ds(first, rows)], target.at[step], sems.at[step])

    def block_of(index):
        return acts.at[index, pl.ds(0, area)]

    def edge_of(index):
        return acts.at[index, pl.ds(area, rows)]

    loads = [
        pltpu.make_async_copy(source, target, load_sem.at[index])
        for index, (source, target) in enumerate(
            (
                (act_hbm, block_of(hi)), (values_hbm, values_ref.at[pl.ds(0, total)]),
                (starts_hbm, starts_ref.at[0]), (back_hbm, back_ref.at[0]),
            )
        )
    ]
    order = list(range(1, groups)) + [0]
    loads[0].start()
    for step in order:
        counts_copy(step, other, counts_raw, raw_sem).start()
    for load in loads[1:]:
        load.start()
    for step in order:
        counts_copy(step, lo, counts, counts_sem).start()

    pl.semaphore_wait(barrier, 1 + hi + lo)

    @pl.when(lo == 1)
    def _():
        pl.semaphore_signal(pair_ready, inc=1, device_id=at(hi, 0, slab), device_id_type=MESH)

    for reach in range(1, groups):

        @pl.when(hi >= reach)
        def _():
            target = jnp.maximum(hi - reach, 0)
            pl.semaphore_signal(
                ready.at[step_of(target)], inc=1, device_id=at(target, lo, slab), device_id_type=MESH
            )

    def line_copies(step):
        return [
            pltpu.make_async_remote_copy(
                src_ref=piece, dst_ref=piece, send_sem=send.at[step], recv_sem=recv.at[step],
                device_id=at(met(step), lo, slab), device_id_type=MESH,
            )
            for piece, send, recv in (
                (block_of(hi), line_send, line_recv), (edge_of(hi), line_edge_send, line_edge_recv)
            )
        ]

    def to_pair(source, target, send, recv):
        return pltpu.make_async_remote_copy(
            src_ref=source, dst_ref=target, send_sem=send, recv_sem=recv,
            device_id=at(hi, other, slab), device_id_type=MESH,
        )

    def to_core(source, target, send, recv):
        return pltpu.make_async_remote_copy(
            src_ref=source, dst_ref=target, send_sem=send, recv_sem=recv,
            device_id=at(hi, lo, 1 - slab), device_id_type=MESH,
        )

    landed = values_ref.at[pl.ds(total + slab * half, half)]
    swaps = [
        to_pair(source, target, swap_send.at[index], swap_recv.at[index])
        for index, (source, target) in enumerate(
            (
                (values_hbm.at[pl.ds(slab * half, half)], landed),
                (starts_hbm, starts_ref.at[1]), (back_hbm, back_ref.at[1]),
            )
        )
    ]
    share = to_core(landed, landed, share_send, share_recv)
    edge_copy = to_core(edge_own, edge_of(hi), edge_send, edge_recv)

    def trade(step):
        return to_pair(counts_out.at[step], counts_in.at[step], trade_send.at[step], trade_recv.at[step])

    def halo_copy(step):
        return to_core(halo_out.at[step], halo_in.at[step], halo_send.at[step], halo_recv.at[step])

    def sum_copies(step):
        return [
            pltpu.make_async_remote_copy(
                src_ref=source.at[step], dst_ref=landing.at[step],
                send_sem=send.at[step], recv_sem=recv.at[step],
                device_id=at(met(step), lo, slab), device_id_type=MESH,
            )
            for source, landing, send, recv in (
                (sum_unit, owner_unit, sum_unit_send, sum_unit_recv),
                (sum_code, owner_code, sum_send, sum_recv),
            )
        ]

    loads[0].wait()
    for reach in range(groups - 1, 0, -1):

        @pl.when(hi >= reach)
        def _():
            line_copies(step_of(jnp.maximum(hi - reach, 0)))[0].start()

    own = acts[hi, :area].astype(jnp.float32).reshape(rows, slices, width)
    edge_own[...] = jnp.where(slab == 0, own[:, slices - 1, :], own[:, 0, :]).astype(jnp.bfloat16)
    edge_copy.start()

    @pl.when(lo == 0)
    def _():
        pl.semaphore_wait(pair_ready, 1)

    for copy in swaps:
        copy.start()

    def send_counts(step):
        counts_copy(step, other, counts_raw, raw_sem).wait()
        counts_out[step] = counts_raw[step].astype(jnp.float32).astype(jnp.bfloat16)
        trade(step).start()

    send_counts(order[0])

    @pl.when(hi < last)
    def _():
        nearest = step_of(jnp.minimum(hi + 1, last))
        pl.semaphore_wait(ready.at[nearest], 1)
        line_copies(nearest)[0].start()

    edge_copy.wait_recv()
    for reach in range(groups - 1, 0, -1):

        @pl.when(hi >= reach)
        def _():
            line_copies(step_of(jnp.maximum(hi - reach, 0)))[1].start()

    @pl.when(hi < last)
    def _():
        line_copies(step_of(jnp.minimum(hi + 1, last)))[1].start()

    def send_rest(place, carry):
        send_counts(lax.rem(place + 1, groups))
        return carry

    lax.fori_loop(1, groups, send_rest, 0)

    def build(which, slot):
        view_index, tap = which // taps, which % taps
        start = starts_ref[slot, tap, view_index : view_index + 1, :]
        turned = jnp.concatenate(
            [values_ref[slot * total + which].astype(jnp.float32), jnp.zeros((8, width), jnp.float32)], axis=0
        )
        shift = 1
        while shift < 8:
            turned = jnp.where((start & shift) != 0, pltpu.roll(turned, shift, axis=0), turned)
            shift *= 2
        while shift < width:
            extra = min(shift, width - turned.shape[0])
            plain = jnp.concatenate([turned, jnp.zeros((extra, width), jnp.float32)], axis=0)
            moved = jnp.concatenate([jnp.zeros((shift, width), jnp.float32), turned], axis=0)[: plain.shape[0]]
            turned = jnp.where((start & shift) != 0, moved, plain)
            shift *= 2
        across = slot * views + view_index
        forward_w[tap * width : (tap + 1) * width, across * width : (across + 1) * width] = (
            turned.astype(jnp.bfloat16)
        )
        backward_w[across * width : (across + 1) * width, tap * width : (tap + 1) * width] = (
            turned.T.astype(jnp.bfloat16)
        )

    for load in loads[1:]:
        load.wait()
    for which in range(total):
        build(which, 0)
    for reach in range(2, groups):

        @pl.when(hi + reach <= last)
        def _():
            later = step_of(jnp.minimum(hi + reach, last))
            pl.semaphore_wait(ready.at[later], 1)
            for copy in line_copies(later):
                copy.start()

    for copy in swaps:
        copy.wait_recv()
    share.start()
    share.wait_recv()
    for which in range(total):
        build(which, 1)

    slice_at = lax.broadcasted_iota(jnp.int32, (rows, slices, width), 1)
    inner = jnp.where(slab == 0, slices - 1, 0)

    def one_group(place, carry):
        step = lax.rem(place + 1, groups)
        group = met(step)

        @pl.when(step > 0)
        def _():
            for copy in line_copies(step):
                copy.wait_recv()

        block = acts[group].astype(jnp.float32)
        image = block[:area].reshape(rows, slices, width)
        edge = block[area:].reshape(rows, 1, width)
        lower = jnp.where(slice_at == 0, jnp.where(slab == 0, 0.0, edge), pltpu.roll(image, 1, axis=1))
        upper = jnp.where(
            slice_at == slices - 1, jnp.where(slab == 0, edge, 0.0), pltpu.roll(image, slices - 1, axis=1)
        )
        stacked = jnp.concatenate(
            [x.reshape(-1, width).astype(jnp.bfloat16) for x in (lower, image, upper)], axis=1
        )
        summed = jnp.dot(stacked, forward_w[...], preferred_element_type=jnp.float32)
        counts_copy(step, lo, counts, counts_sem).wait()
        trade(step).wait_recv()
        ratios = []
        ratio_edges = []
        for across in range(PAIR * views):
            slot, view_index = across // views, across % views
            expected = (
                summed[:, across * width : (across + 1) * width].reshape(rows, slices, width)
                + back_ref[slot, view_index].astype(jnp.float32)[None]
            )
            events = (counts_in if slot else counts)[step, view_index].astype(jnp.float32)
            ratio = events / expected - 1.0
            ratio_edges.append(
                jnp.where(slab == 0, ratio[:, slices - 1, :], ratio[:, 0, :]).astype(jnp.bfloat16)
            )
            ratios.append(ratio.reshape(-1, width).astype(jnp.bfloat16))
        outer = pl.multiple_of((1 - slab) * ((taps - 1) * width), width)
        halo_out[step] = jnp.dot(
            jnp.concatenate(ratio_edges, axis=1), backward_w[:, pl.ds(outer, width)],
            preferred_element_type=jnp.float32,
        )
        halo_copy(step).start()
        spread = jnp.dot(
            jnp.concatenate(ratios, axis=1), backward_w[...], preferred_element_type=jnp.float32
        ).reshape(rows, slices, taps * width)
        from_upper = pltpu.roll(spread[:, :, :width], slices - 1, axis=1)
        from_lower = pltpu.roll(spread[:, :, 2 * width :], 1, axis=1)
        from_upper = jnp.where(slice_at == slices - 1, 0.0, from_upper)
        from_lower = jnp.where(slice_at == 0, 0.0, from_lower)
        whole[...] = spread[:, :, width : 2 * width] + from_upper + from_lower
        halo_copy(step).wait_recv()
        whole[...] += jnp.where(slice_at == inner, halo_in[step].reshape(rows, 1, width), 0.0)

        @pl.when(step > 0)
        def _():
            sum_code[step], sum_unit[step] = encode(whole[...])
            for copy in sum_copies(step):
                copy.start()

        return carry

    lax.fori_loop(0, groups, one_group, 0)
    for step in range(1, groups):
        for copy in sum_copies(step):
            copy.wait_recv()
        whole[...] += decode(owner_code[step], owner_unit[step])
    out_ref[...] = whole[...]

    for copy in swaps:
        copy.wait_send()
    share.wait_send()
    edge_copy.wait_send()
    for step in range(groups):
        halo_copy(step).wait_send()
        trade(step).wait_send()
    for step in range(1, groups):
        for copy in line_copies(step) + sum_copies(step):
            copy.wait_send()


def per_device(activity, histo_counts, background, blur_values, band_start):
    members = lax.axis_size("view")
    groups = members // PAIR
    rows, slices, width = activity.shape
    views, taps, _, band = blur_values.shape
    area = rows * slices
    total = views * taps
    dma = pltpu.SemaphoreType.DMA
    block = (rows, slices, width)
    shared = (groups, views) + block
    unit = (groups, 1, width)
    return pl.pallas_call(
        functools.partial(kernel, groups),
        out_shape=jax.ShapeDtypeStruct(block, jnp.float32),
        in_specs=[pl.BlockSpec(memory_space=pl.ANY)] * 5,
        out_specs=pl.BlockSpec(memory_space=pltpu.VMEM),
        scratch_shapes=[
            pltpu.VMEM((PAIR,) + background.shape, jnp.bfloat16),
            pltpu.VMEM((PAIR * total, band, width), jnp.bfloat16),
            pltpu.VMEM((PAIR, taps, views, width), jnp.int32),
            pltpu.VMEM((groups, area + rows, width), jnp.bfloat16),
            pltpu.VMEM((rows, width), jnp.bfloat16),
            pltpu.VMEM(shared, jnp.int32),
            pltpu.VMEM(shared, jnp.int32),
            pltpu.VMEM(shared, jnp.bfloat16),
            pltpu.VMEM(shared, jnp.bfloat16),
            pltpu.VMEM((taps * width, PAIR * views * width), jnp.bfloat16),
            pltpu.VMEM((PAIR * views * width, taps * width), jnp.bfloat16),
            pltpu.VMEM(block, jnp.float32),
            pltpu.VMEM((groups,) + block, jnp.int16),
            pltpu.VMEM(unit, jnp.float32),
            pltpu.VMEM((groups,) + block, jnp.int16),
            pltpu.VMEM(unit, jnp.float32),
            pltpu.VMEM((groups, rows, width), jnp.float32),
            pltpu.VMEM((groups, rows, width), jnp.float32),
            dma((4,)),
            dma((groups,)), dma((groups,)),
            pltpu.SemaphoreType.REGULAR((groups,)),
            pltpu.SemaphoreType.REGULAR,
            dma((groups,)), dma((groups,)), dma((groups,)), dma((groups,)),
            dma((3,)), dma((3,)), dma, dma, dma((groups,)), dma((groups,)),
            dma, dma, dma((groups,)), dma((groups,)),
            dma((groups,)), dma((groups,)), dma((groups,)), dma((groups,)),
        ],
        compiler_params=pltpu.CompilerParams(collective_id=0, has_side_effects=True, vmem_limit_bytes=VMEM_LIMIT),
        name="poisson_gradient",
    )(
        activity.reshape(area, width), histo_counts, background,
        jnp.swapaxes(blur_values, 2, 3).reshape(total, band, width), jnp.swapaxes(band_start, 0, 1),
    )


def solution(mesh):
    placed = (
        P(("parts", "view"), "slab", None),
        P(("parts", "view"), None, "slab", None),
        P(("parts", "view"), "slab", None),
        P("view", None, None, None),
        P("view", None, None),
    )
    return jax.shard_map(
        per_device,
        mesh=mesh,
        in_specs=placed,
        out_specs=P(("parts", "view"), "slab", None),
        check_vma=False,
    )
```

```python
import functools

import jax
import jax.numpy as jnp
from jax import lax
from jax.experimental import pallas as pl
from jax.experimental.pallas import tpu as pltpu
from jax.sharding import PartitionSpec as P

MESH = pl.DeviceIdType.MESH
PAIR = 2


CODE_MAX = 32767.0
TINY = 1e-30
VMEM_LIMIT = 63 << 20


def encode(block):
    top = jnp.max(jnp.abs(block), axis=(0, 1), keepdims=False)[None, :]
    scale = jnp.where(top > TINY, CODE_MAX / jnp.maximum(top, TINY), 0.0)
    code = jnp.round(block * scale[None]).astype(jnp.int32).astype(jnp.int16)
    return code, top * (1.0 / CODE_MAX)


def decode(code, unit):
    return code.astype(jnp.int32).astype(jnp.float32) * unit[None]


def kernel(
    groups, act_hbm, counts_hbm, back_hbm, values_hbm, starts_hbm, out_ref,
    back_ref, values_ref, starts_ref,
    acts, edge_own, counts, counts_raw, counts_out, counts_in, forward_w, backward_w, summed, spread_own, whole,
    sum_code, sum_unit, owner_code, owner_unit, halo_out, halo_in,
    load_sem, counts_sem, raw_sem, ready, pair_ready, line_send, line_recv, line_edge_send, line_edge_recv,
    swap_send, swap_recv, share_send, share_recv, trade_send, trade_recv,
    edge_send, edge_recv, halo_send, halo_recv, sum_send, sum_recv, sum_unit_send, sum_unit_recv,
):
    part = lax.axis_index("parts")
    view = lax.axis_index("view")
    slab = lax.axis_index("slab")
    last = groups - 1
    hi = view // PAIR
    lo = view % PAIR
    other = 1 - lo
    rows, slices, width = out_ref.shape
    area = rows * slices
    views = back_hbm.shape[0]
    total = values_hbm.shape[0]
    taps = total // views
    half = total // 2

    def at(hi_index, lo_index, slab_index):
        return (part, hi_index * PAIR + lo_index, slab_index)

    def group_at(place):
        return jnp.where(place == last, hi, jnp.where(place < hi, place, place + 1))

    barrier = pltpu.get_barrier_semaphore()
    pl.semaphore_signal(barrier, inc=1, device_id=at(hi, lo, 1 - slab), device_id_type=MESH)

    @pl.when(lo == 0)
    def _():
        pl.semaphore_signal(barrier, inc=1, device_id=at(hi, 1, slab), device_id_type=MESH)

    for index in range(1, groups):

        @pl.when(index > hi)
        def _():
            pl.semaphore_signal(barrier, inc=1, device_id=at(index, lo, slab), device_id_type=MESH)

    def counts_copy(place, column, target, sems):
        first = pl.multiple_of((group_at(place) * PAIR + column) * rows, rows)
        return pltpu.make_async_copy(counts_hbm.at[:, pl.ds(first, rows)], target.at[place], sems.at[place])

    def block_of(index):
        return acts.at[index, pl.ds(0, area)]

    def edge_of(index):
        return acts.at[index, pl.ds(area, rows)]

    loads = [
        pltpu.make_async_copy(source, target, load_sem.at[index])
        for index, (source, target) in enumerate(
            (
                (act_hbm, block_of(hi)), (values_hbm, values_ref.at[pl.ds(0, total)]),
                (starts_hbm, starts_ref.at[0]), (back_hbm, back_ref.at[0]),
            )
        )
    ]
    loads[0].start()
    for place in range(groups):
        counts_copy(place, other, counts_raw, raw_sem).start()
    for load in loads[1:]:
        load.start()
    for place in range(groups):
        counts_copy(place, lo, counts, counts_sem).start()

    pl.semaphore_wait(barrier, 1 + hi + lo)

    @pl.when(lo == 1)
    def _():
        pl.semaphore_signal(pair_ready, inc=1, device_id=at(hi, 0, slab), device_id_type=MESH)

    for target in range(last):

        @pl.when(target < hi)
        def _():
            pl.semaphore_signal(ready.at[hi], inc=1, device_id=at(target, lo, slab), device_id_type=MESH)

    def line_copy(target, piece, send, recv, source):
        return pltpu.make_async_remote_copy(
            src_ref=piece(hi), dst_ref=piece(hi), send_sem=send.at[target], recv_sem=recv.at[source],
            device_id=at(target, lo, slab), device_id_type=MESH,
        )

    def block_copy(target, source=hi):
        return line_copy(target, block_of, line_send, line_recv, source)

    def rim_copy(target, source=hi):
        return line_copy(target, edge_of, line_edge_send, line_edge_recv, source)

    def to_pair(source, target, send, recv):
        return pltpu.make_async_remote_copy(
            src_ref=source, dst_ref=target, send_sem=send, recv_sem=recv,
            device_id=at(hi, other, slab), device_id_type=MESH,
        )

    def to_core(source, target, send, recv):
        return pltpu.make_async_remote_copy(
            src_ref=source, dst_ref=target, send_sem=send, recv_sem=recv,
            device_id=at(hi, lo, 1 - slab), device_id_type=MESH,
        )

    landed = values_ref.at[pl.ds(total + slab * half, half)]
    swaps = [
        to_pair(source, target, swap_send.at[index], swap_recv.at[index])
        for index, (source, target) in enumerate(
            (
                (values_hbm.at[pl.ds(slab * half, half)], landed),
                (starts_hbm, starts_ref.at[1]), (back_hbm, back_ref.at[1]),
            )
        )
    ]
    share = to_core(landed, landed, share_send, share_recv)
    edge_copy = to_core(edge_own, edge_of(hi), edge_send, edge_recv)

    def trade(place):
        return to_pair(counts_out.at[place], counts_in.at[place], trade_send.at[place], trade_recv.at[place])

    def halo_copy(place):
        return to_core(halo_out.at[place], halo_in.at[place], halo_send.at[place], halo_recv.at[place])

    def sum_copies(target, source=hi):
        return [
            pltpu.make_async_remote_copy(
                src_ref=out.at[target], dst_ref=landing.at[hi], send_sem=send.at[target], recv_sem=recv.at[source],
                device_id=at(target, lo, slab), device_id_type=MESH,
            )
            for out, landing, send, recv in (
                (sum_unit, owner_unit, sum_unit_send, sum_unit_recv),
                (sum_code, owner_code, sum_send, sum_recv),
            )
        ]

    @pl.when(lo == 1)
    def _():
        for copy in swaps:
            copy.start()

    loads[0].wait()
    for target in range(last):

        @pl.when(target < hi)
        def _():
            block_copy(target).start()

    own = acts[hi, :area].astype(jnp.float32).reshape(rows, slices, width)
    edge_own[...] = jnp.where(slab == 0, own[:, slices - 1, :], own[:, 0, :]).astype(jnp.bfloat16)
    edge_copy.start()

    def send_counts(place):
        counts_copy(place, other, counts_raw, raw_sem).wait()
        counts_out[place] = counts_raw[place].astype(jnp.float32).astype(jnp.bfloat16)
        trade(place).start()

    @pl.when(lo == 0)
    def _():
        pl.semaphore_wait(pair_ready, 1)
        for copy in swaps:
            copy.start()

    send_counts(0)

    @pl.when(hi < last)
    def _():
        pl.semaphore_wait(ready.at[hi + 1], 1)
        block_copy(hi + 1).start()

    edge_copy.wait_recv()
    for target in range(last):

        @pl.when(target < hi)
        def _():
            rim_copy(target).start()

    @pl.when(hi < last)
    def _():
        rim_copy(hi + 1).start()

    def send_rest(place, carry):
        send_counts(place)
        return carry

    lax.fori_loop(1, groups, send_rest, 0)

    def build(which, slot):
        view_index, tap = which // taps, which % taps
        start = starts_ref[slot, tap, view_index : view_index + 1, :]
        turned = jnp.concatenate(
            [values_ref[slot * total + which].astype(jnp.float32), jnp.zeros((8, width), jnp.float32)], axis=0
        )
        shift = 1
        while shift < 8:
            turned = jnp.where((start & shift) != 0, pltpu.roll(turned, shift, axis=0), turned)
            shift *= 2
        while shift < width:
            extra = min(shift, width - turned.shape[0])
            plain = jnp.concatenate([turned, jnp.zeros((extra, width), jnp.float32)], axis=0)
            moved = jnp.concatenate([jnp.zeros((shift, width), jnp.float32), turned], axis=0)[: plain.shape[0]]
            turned = jnp.where((start & shift) != 0, moved, plain)
            shift *= 2
        place = slot * views + view_index
        forward_w[tap * width : (tap + 1) * width, place * width : (place + 1) * width] = (
            turned.astype(jnp.bfloat16)
        )
        backward_w[place * width : (place + 1) * width, tap * width : (tap + 1) * width] = (
            turned.T.astype(jnp.bfloat16)
        )

    for load in loads[1:]:
        load.wait()
    for which in range(total):
        build(which, 0)
    for target in range(2, groups):

        @pl.when(target > hi + 1)
        def _():
            pl.semaphore_wait(ready.at[target], 1)
            block_copy(target).start()
            rim_copy(target).start()

    for copy in swaps:
        copy.wait_recv()
    share.start()
    share.wait_recv()
    for which in range(total):
        build(which, 1)

    slice_at = lax.broadcasted_iota(jnp.int32, (rows, slices, width), 1)
    inner = jnp.where(slab == 0, slices - 1, 0)

    across = views * width
    outer = pl.multiple_of((1 - slab) * ((taps - 1) * width), width)

    def one_group(place, carry):
        group = group_at(place)

        @pl.when(place < last)
        def _():
            block_copy(group, group).wait_recv()
            rim_copy(group, group).wait_recv()

        block = acts[group].astype(jnp.float32)
        image = block[:area].reshape(rows, slices, width)
        edge = block[area:].reshape(rows, 1, width)
        lower = jnp.where(slice_at == 0, jnp.where(slab == 0, 0.0, edge), pltpu.roll(image, 1, axis=1))
        upper = jnp.where(
            slice_at == slices - 1, jnp.where(slab == 0, edge, 0.0), pltpu.roll(image, slices - 1, axis=1)
        )
        stacked = jnp.concatenate(
            [x.reshape(-1, width).astype(jnp.bfloat16) for x in (lower, image, upper)], axis=1
        )
        summed[...] = jnp.dot(stacked, forward_w[...], preferred_element_type=jnp.float32)

        def ratios_of(slot, events):
            ratios = []
            ratio_edges = []
            for view_index in range(views):
                first = slot * across + view_index * width
                expected = (
                    summed[:, first : first + width].reshape(rows, slices, width)
                    + back_ref[slot, view_index].astype(jnp.float32)[None]
                )
                ratio = events[place, view_index].astype(jnp.float32) / expected - 1.0
                ratio_edges.append(
                    jnp.where(slab == 0, ratio[:, slices - 1, :], ratio[:, 0, :]).astype(jnp.bfloat16)
                )
                ratios.append(ratio.reshape(-1, width).astype(jnp.bfloat16))
            return jnp.concatenate(ratios, axis=1), jnp.concatenate(ratio_edges, axis=1)

        counts_copy(place, lo, counts, counts_sem).wait()
        ratios, ratio_edges = ratios_of(0, counts)
        halo_out[place] = jnp.dot(
            ratio_edges, backward_w[:across, pl.ds(outer, width)], preferred_element_type=jnp.float32
        )
        spread_own[...] = jnp.dot(ratios, backward_w[:across], preferred_element_type=jnp.float32)
        trade(place).wait_recv()
        ratios, ratio_edges = ratios_of(1, counts_in)
        halo_out[place] += jnp.dot(
            ratio_edges, backward_w[across:, pl.ds(outer, width)], preferred_element_type=jnp.float32
        )
        halo_copy(place).start()
        spread = (
            spread_own[...] + jnp.dot(ratios, backward_w[across:], preferred_element_type=jnp.float32)
        ).reshape(rows, slices, taps * width)
        from_upper = pltpu.roll(spread[:, :, :width], slices - 1, axis=1)
        from_lower = pltpu.roll(spread[:, :, 2 * width :], 1, axis=1)
        from_upper = jnp.where(slice_at == slices - 1, 0.0, from_upper)
        from_lower = jnp.where(slice_at == 0, 0.0, from_lower)
        whole[...] = spread[:, :, width : 2 * width] + from_upper + from_lower
        halo_copy(place).wait_recv()
        whole[...] += jnp.where(slice_at == inner, halo_in[place].reshape(rows, 1, width), 0.0)

        @pl.when(place < last)
        def _():
            sum_code[group], sum_unit[group] = encode(whole[...])
            for copy in sum_copies(group):
                copy.start()

        return carry

    lax.fori_loop(0, groups, one_group, 0)
    for place in range(last):
        source = group_at(place)
        for copy in sum_copies(source, source):
            copy.wait_recv()
        whole[...] += decode(owner_code[source], owner_unit[source])
    out_ref[...] = whole[...]

    for copy in swaps:
        copy.wait_send()
    share.wait_send()
    edge_copy.wait_send()
    for place in range(groups):
        halo_copy(place).wait_send()
        trade(place).wait_send()
    for place in range(last):
        target = group_at(place)
        block_copy(target).wait_send()
        rim_copy(target).wait_send()
        for copy in sum_copies(target):
            copy.wait_send()


def per_device(activity, histo_counts, background, blur_values, band_start):
    members = lax.axis_size("view")
    groups = members // PAIR
    rows, slices, width = activity.shape
    views, taps, _, band = blur_values.shape
    area = rows * slices
    total = views * taps
    dma = pltpu.SemaphoreType.DMA
    block = (rows, slices, width)
    shared = (groups, views) + block
    unit = (groups, 1, width)
    return pl.pallas_call(
        functools.partial(kernel, groups),
        out_shape=pltpu.VMEM(block, jnp.float32),
        in_specs=[pl.BlockSpec(memory_space=pl.ANY)] * 5,
        out_specs=pl.BlockSpec(memory_space=pltpu.VMEM),
        scratch_shapes=[
            pltpu.VMEM((PAIR,) + background.shape, jnp.bfloat16),
            pltpu.VMEM((PAIR * total, band, width), jnp.bfloat16),
            pltpu.VMEM((PAIR, taps, views, width), jnp.int32),
            pltpu.VMEM((groups, area + rows, width), jnp.bfloat16),
            pltpu.VMEM((rows, width), jnp.bfloat16),
            pltpu.VMEM(shared, jnp.int32),
            pltpu.VMEM(shared, jnp.int32),
            pltpu.VMEM(shared, jnp.bfloat16),
            pltpu.VMEM(shared, jnp.bfloat16),
            pltpu.VMEM((taps * width, PAIR * views * width), jnp.bfloat16),
            pltpu.VMEM((PAIR * views * width, taps * width), jnp.bfloat16),
            pltpu.VMEM((area, PAIR * views * width), jnp.float32),
            pltpu.VMEM((area, taps * width), jnp.float32),
            pltpu.VMEM(block, jnp.float32),
            pltpu.VMEM((groups,) + block, jnp.int16),
            pltpu.VMEM(unit, jnp.float32),
            pltpu.VMEM((groups,) + block, jnp.int16),
            pltpu.VMEM(unit, jnp.float32),
            pltpu.VMEM((groups, rows, width), jnp.float32),
            pltpu.VMEM((groups, rows, width), jnp.float32),
            dma((4,)),
            dma((groups,)), dma((groups,)),
            pltpu.SemaphoreType.REGULAR((groups,)),
            pltpu.SemaphoreType.REGULAR,
            dma((groups,)), dma((groups,)), dma((groups,)), dma((groups,)),
            dma((3,)), dma((3,)), dma, dma, dma((groups,)), dma((groups,)),
            dma, dma, dma((groups,)), dma((groups,)),
            dma((groups,)), dma((groups,)), dma((groups,)), dma((groups,)),
        ],
        compiler_params=pltpu.CompilerParams(collective_id=0, has_side_effects=True, vmem_limit_bytes=VMEM_LIMIT),
        name="poisson_gradient",
    )(
        activity.reshape(area, width), histo_counts, background,
        jnp.swapaxes(blur_values, 2, 3).reshape(total, band, width), jnp.swapaxes(band_start, 0, 1),
    )


def solution(mesh):
    placed = (
        P(("parts", "view"), "slab", None),
        P(("parts", "view"), None, "slab", None),
        P(("parts", "view"), "slab", None),
        P("view", None, None, None),
        P("view", None, None),
    )
    return jax.shard_map(
        per_device,
        mesh=mesh,
        in_specs=placed,
        out_specs=P(("parts", "view"), "slab", None),
        check_vma=False,
    )
```

```python
import functools

import jax
import jax.numpy as jnp
from jax import lax
from jax.experimental import pallas as pl
from jax.experimental.pallas import tpu as pltpu
from jax.sharding import PartitionSpec as P

MESH = pl.DeviceIdType.MESH
PAIR = 2


CODE_MAX = 32767.0
TINY = 1e-30
VMEM_LIMIT = 63 << 20


def encode(block):
    top = jnp.max(jnp.abs(block), axis=(0, 1), keepdims=False)[None, :]
    scale = jnp.where(top > TINY, CODE_MAX / jnp.maximum(top, TINY), 0.0)
    code = jnp.round(block * scale[None]).astype(jnp.int32).astype(jnp.int16)
    return code, top * (1.0 / CODE_MAX)


def decode(code, unit):
    return code.astype(jnp.int32).astype(jnp.float32) * unit[None]


def kernel(
    groups, act_hbm, counts_hbm, back_hbm, values_hbm, starts_hbm, out_ref,
    back_ref, values_ref, starts_ref,
    acts, edge_own, counts, counts_raw, counts_out, counts_in, forward_w, backward_w, summed, spread_own, whole,
    sum_code, sum_unit, owner_code, owner_unit, halo_out, halo_in,
    load_sem, counts_sem, raw_sem, ready, pair_ready, line_send, line_recv, line_edge_send, line_edge_recv,
    swap_send, swap_recv, share_send, share_recv, trade_send, trade_recv,
    edge_send, edge_recv, halo_send, halo_recv, sum_send, sum_recv, sum_unit_send, sum_unit_recv,
):
    part = lax.axis_index("parts")
    view = lax.axis_index("view")
    slab = lax.axis_index("slab")
    last = groups - 1
    hi = view // PAIR
    lo = view % PAIR
    other = 1 - lo
    rows, slices, width = out_ref.shape
    area = rows * slices
    views = back_hbm.shape[0]
    total = values_hbm.shape[0]
    taps = total // views

    def at(hi_index, lo_index, slab_index):
        return (part, hi_index * PAIR + lo_index, slab_index)

    def group_at(place):
        rank = last - place
        both = jnp.minimum(hi, last - hi)
        inward = jnp.where(hi < last - hi, 1, -1)
        reach = (rank + 1) // 2
        around = jnp.where(rank % 2 == 1, hi + inward * reach, hi - inward * reach)
        beyond = jnp.where(hi < last - hi, rank, place)
        return jnp.where(rank <= 2 * both, around, beyond)

    barrier = pltpu.get_barrier_semaphore()
    pl.semaphore_signal(barrier, inc=1, device_id=at(hi, lo, 1 - slab), device_id_type=MESH)

    @pl.when(lo == 0)
    def _():
        pl.semaphore_signal(barrier, inc=1, device_id=at(hi, 1, slab), device_id_type=MESH)

    for index in range(1, groups):

        @pl.when(index > hi)
        def _():
            pl.semaphore_signal(barrier, inc=1, device_id=at(index, lo, slab), device_id_type=MESH)

    def counts_copy(place, column, target, sems):
        first = pl.multiple_of((group_at(place) * PAIR + column) * rows, rows)
        return pltpu.make_async_copy(counts_hbm.at[:, pl.ds(first, rows)], target.at[place], sems.at[place])

    def block_of(index):
        return acts.at[index, pl.ds(0, area)]

    def edge_of(index):
        return acts.at[index, pl.ds(area, rows)]

    loads = [
        pltpu.make_async_copy(source, target, load_sem.at[index])
        for index, (source, target) in enumerate(
            (
                (act_hbm, block_of(hi)), (values_hbm, values_ref.at[pl.ds(0, total)]),
                (starts_hbm, starts_ref.at[0]), (back_hbm, back_ref.at[0]),
            )
        )
    ]
    loads[0].start()
    for place in range(groups):
        counts_copy(place, other, counts_raw, raw_sem).start()
    for load in loads[1:]:
        load.start()
    for place in range(groups):
        counts_copy(place, lo, counts, counts_sem).start()

    pl.semaphore_wait(barrier, 1 + hi + lo)


    @pl.when(lo == 1)
    def _():
        pl.semaphore_signal(pair_ready, inc=1, device_id=at(hi, 0, slab), device_id_type=MESH)

    for target in range(last):

        @pl.when(target < hi)
        def _():
            pl.semaphore_signal(ready.at[hi], inc=1, device_id=at(target, lo, slab), device_id_type=MESH)

    def line_copy(target, piece, send, recv, source):
        return pltpu.make_async_remote_copy(
            src_ref=piece(hi), dst_ref=piece(hi), send_sem=send.at[target], recv_sem=recv.at[source],
            device_id=at(target, lo, slab), device_id_type=MESH,
        )

    def block_copy(target, source=hi):
        return line_copy(target, block_of, line_send, line_recv, source)

    def rim_copy(target, source=hi):
        return line_copy(target, edge_of, line_edge_send, line_edge_recv, source)

    def to_pair(source, target, send, recv):
        return pltpu.make_async_remote_copy(
            src_ref=source, dst_ref=target, send_sem=send, recv_sem=recv,
            device_id=at(hi, other, slab), device_id_type=MESH,
        )

    def to_core(source, target, send, recv):
        return pltpu.make_async_remote_copy(
            src_ref=source, dst_ref=target, send_sem=send, recv_sem=recv,
            device_id=at(hi, lo, 1 - slab), device_id_type=MESH,
        )

    bands = [
        to_pair(source, target, swap_send.at[index], swap_recv.at[index])
        for index, (source, target) in enumerate(
            ((values_hbm, values_ref.at[pl.ds(total, total)]), (starts_hbm, starts_ref.at[1]))
        )
    ]
    shares = [
        to_core(target, target, share_send.at[index], share_recv.at[index])
        for index, target in enumerate((values_ref.at[pl.ds(total, total)], starts_ref.at[1]))
    ]
    level_copy = to_pair(back_hbm, back_ref.at[1], swap_send.at[2], swap_recv.at[2])

    def start_swaps():
        @pl.when(slab == 1)
        def _():
            for copy in bands:
                copy.start()

        level_copy.start()

    edge_copy = to_core(edge_own, edge_of(hi), edge_send, edge_recv)

    def trade(place):
        return to_pair(counts_out.at[place], counts_in.at[place], trade_send.at[place], trade_recv.at[place])

    def halo_copy(place):
        return to_core(halo_out.at[place], halo_in.at[place], halo_send.at[place], halo_recv.at[place])

    def sum_copies(target, source=hi):
        return [
            pltpu.make_async_remote_copy(
                src_ref=out.at[target], dst_ref=landing.at[hi], send_sem=send.at[target], recv_sem=recv.at[source],
                device_id=at(target, lo, slab), device_id_type=MESH,
            )
            for out, landing, send, recv in (
                (sum_unit, owner_unit, sum_unit_send, sum_unit_recv),
                (sum_code, owner_code, sum_send, sum_recv),
            )
        ]

    @pl.when(lo == 1)
    def _():
        start_swaps()

    loads[0].wait()
    for target in range(last):

        @pl.when(target < hi)
        def _():
            block_copy(target).start()

    own = acts[hi, :area].astype(jnp.float32).reshape(rows, slices, width)
    edge_own[...] = jnp.where(slab == 0, own[:, slices - 1, :], own[:, 0, :]).astype(jnp.bfloat16)
    edge_copy.start()

    def send_counts(place):
        counts_copy(place, other, counts_raw, raw_sem).wait()
        counts_out[place] = counts_raw[place].astype(jnp.float32).astype(jnp.bfloat16)
        trade(place).start()

    @pl.when(lo == 0)
    def _():
        pl.semaphore_wait(pair_ready, 1)
        start_swaps()

    send_counts(0)

    @pl.when(hi < last)
    def _():
        pl.semaphore_wait(ready.at[hi + 1], 1)
        block_copy(hi + 1).start()

    edge_copy.wait_recv()
    for target in range(last):

        @pl.when(target < hi)
        def _():
            rim_copy(target).start()

    @pl.when(hi < last)
    def _():
        rim_copy(hi + 1).start()

    def send_rest(place, carry):
        send_counts(place)
        return carry

    lax.fori_loop(1, groups, send_rest, 0)

    def build(which, slot):
        view_index, tap = which // taps, which % taps
        start = starts_ref[slot, tap, view_index : view_index + 1, :]
        turned = jnp.concatenate(
            [values_ref[slot * total + which].astype(jnp.float32), jnp.zeros((8, width), jnp.float32)], axis=0
        )
        shift = 1
        while shift < 8:
            turned = jnp.where((start & shift) != 0, pltpu.roll(turned, shift, axis=0), turned)
            shift *= 2
        while shift < width:
            extra = min(shift, width - turned.shape[0])
            plain = jnp.concatenate([turned, jnp.zeros((extra, width), jnp.float32)], axis=0)
            moved = jnp.concatenate([jnp.zeros((shift, width), jnp.float32), turned], axis=0)[: plain.shape[0]]
            turned = jnp.where((start & shift) != 0, moved, plain)
            shift *= 2
        place = slot * views + view_index
        forward_w[tap * width : (tap + 1) * width, place * width : (place + 1) * width] = (
            turned.astype(jnp.bfloat16)
        )
        backward_w[place * width : (place + 1) * width, tap * width : (tap + 1) * width] = (
            turned.T.astype(jnp.bfloat16)
        )

    for load in loads[1:]:
        load.wait()
    for which in range(total):
        build(which, 0)
    for target in range(2, groups):

        @pl.when(target > hi + 1)
        def _():
            pl.semaphore_wait(ready.at[target], 1)
            block_copy(target).start()
            rim_copy(target).start()


    @pl.when(slab == 1)
    def _():
        for index in range(2):
            bands[index].wait_recv()
            shares[index].start()

    @pl.when(slab == 0)
    def _():
        for copy in shares:
            copy.wait_recv()

    level_copy.wait_recv()
    for which in range(total):
        build(which, 1)

    slice_at = lax.broadcasted_iota(jnp.int32, (rows, slices, width), 1)
    inner = jnp.where(slab == 0, slices - 1, 0)

    across = views * width
    outer = pl.multiple_of((1 - slab) * ((taps - 1) * width), width)

    def one_group(place, carry):
        group = group_at(place)

        @pl.when(place < last)
        def _():
            block_copy(group, group).wait_recv()
            rim_copy(group, group).wait_recv()

        block = acts[group].astype(jnp.float32)
        image = block[:area].reshape(rows, slices, width)
        edge = block[area:].reshape(rows, 1, width)
        lower = jnp.where(slice_at == 0, jnp.where(slab == 0, 0.0, edge), pltpu.roll(image, 1, axis=1))
        upper = jnp.where(
            slice_at == slices - 1, jnp.where(slab == 0, edge, 0.0), pltpu.roll(image, slices - 1, axis=1)
        )
        stacked = jnp.concatenate(
            [x.reshape(-1, width).astype(jnp.bfloat16) for x in (lower, image, upper)], axis=1
        )
        summed[...] = jnp.dot(stacked, forward_w[...], preferred_element_type=jnp.float32)

        @pl.when((place == last) & (slab == 1))
        def _():
            for copy in bands + shares:
                copy.wait_send()

        @pl.when(place == last)
        def _():
            level_copy.wait_send()
            edge_copy.wait_send()
            for done in range(last):
                target = group_at(done)
                halo_copy(done).wait_send()
                trade(done).wait_send()
                block_copy(target).wait_send()
                rim_copy(target).wait_send()
                if done < last - 1:
                    for copy in sum_copies(target):
                        copy.wait_send()


        def ratios_of(slot, events):
            ratios = []
            ratio_edges = []
            for view_index in range(views):
                first = slot * across + view_index * width
                expected = (
                    summed[:, first : first + width].reshape(rows, slices, width)
                    + back_ref[slot, view_index].astype(jnp.float32)[None]
                )
                ratio = events[place, view_index].astype(jnp.float32) / expected - 1.0
                ratio_edges.append(
                    jnp.where(slab == 0, ratio[:, slices - 1, :], ratio[:, 0, :]).astype(jnp.bfloat16)
                )
                ratios.append(ratio.reshape(-1, width).astype(jnp.bfloat16))
            return jnp.concatenate(ratios, axis=1), jnp.concatenate(ratio_edges, axis=1)

        counts_copy(place, lo, counts, counts_sem).wait()
        ratios, ratio_edges = ratios_of(0, counts)
        halo_out[place] = jnp.dot(
            ratio_edges, backward_w[:across, pl.ds(outer, width)], preferred_element_type=jnp.float32
        )
        spread_own[...] = jnp.dot(ratios, backward_w[:across], preferred_element_type=jnp.float32)
        trade(place).wait_recv()
        ratios, ratio_edges = ratios_of(1, counts_in)
        halo_out[place] += jnp.dot(
            ratio_edges, backward_w[across:, pl.ds(outer, width)], preferred_element_type=jnp.float32
        )
        halo_copy(place).start()
        spread = (
            spread_own[...] + jnp.dot(ratios, backward_w[across:], preferred_element_type=jnp.float32)
        ).reshape(rows, slices, taps * width)
        from_upper = pltpu.roll(spread[:, :, :width], slices - 1, axis=1)
        from_lower = pltpu.roll(spread[:, :, 2 * width :], 1, axis=1)
        from_upper = jnp.where(slice_at == slices - 1, 0.0, from_upper)
        from_lower = jnp.where(slice_at == 0, 0.0, from_lower)
        whole[...] = spread[:, :, width : 2 * width] + from_upper + from_lower
        halo_copy(place).wait_recv()
        whole[...] += jnp.where(slice_at == inner, halo_in[place].reshape(rows, 1, width), 0.0)

        @pl.when(place < last)
        def _():
            sum_code[group], sum_unit[group] = encode(whole[...])
            for copy in sum_copies(group):
                copy.start()

        return carry

    lax.fori_loop(0, groups, one_group, 0)
    for place in range(last):
        source = group_at(place)
        for copy in sum_copies(source, source):
            copy.wait_recv()
        whole[...] += decode(owner_code[source], owner_unit[source])
    out_ref[...] = whole[...]

    halo_copy(last).wait_send()
    trade(last).wait_send()
    for copy in sum_copies(group_at(last - 1)):
        copy.wait_send()


def per_device(activity, histo_counts, background, blur_values, band_start):
    members = lax.axis_size("view")
    groups = members // PAIR
    rows, slices, width = activity.shape
    views, taps, _, band = blur_values.shape
    area = rows * slices
    total = views * taps
    dma = pltpu.SemaphoreType.DMA
    block = (rows, slices, width)
    shared = (groups, views) + block
    unit = (groups, 1, width)
    return pl.pallas_call(
        functools.partial(kernel, groups),
        out_shape=pltpu.VMEM(block, jnp.float32),
        in_specs=[pl.BlockSpec(memory_space=pl.ANY)] * 5,
        out_specs=pl.BlockSpec(memory_space=pltpu.VMEM),
        scratch_shapes=[
            pltpu.VMEM((PAIR,) + background.shape, jnp.bfloat16),
            pltpu.VMEM((PAIR * total, band, width), jnp.bfloat16),
            pltpu.VMEM((PAIR, taps, views, width), jnp.int32),
            pltpu.VMEM((groups, area + rows, width), jnp.bfloat16),
            pltpu.VMEM((rows, width), jnp.bfloat16),
            pltpu.VMEM(shared, jnp.int32),
            pltpu.VMEM(shared, jnp.int32),
            pltpu.VMEM(shared, jnp.bfloat16),
            pltpu.VMEM(shared, jnp.bfloat16),
            pltpu.VMEM((taps * width, PAIR * views * width), jnp.bfloat16),
            pltpu.VMEM((PAIR * views * width, taps * width), jnp.bfloat16),
            pltpu.VMEM((area, PAIR * views * width), jnp.float32),
            pltpu.VMEM((area, taps * width), jnp.float32),
            pltpu.VMEM(block, jnp.float32),
            pltpu.VMEM((groups,) + block, jnp.int16),
            pltpu.VMEM(unit, jnp.float32),
            pltpu.VMEM((groups,) + block, jnp.int16),
            pltpu.VMEM(unit, jnp.float32),
            pltpu.VMEM((groups, rows, width), jnp.float32),
            pltpu.VMEM((groups, rows, width), jnp.float32),
            dma((4,)),
            dma((groups,)), dma((groups,)),
            pltpu.SemaphoreType.REGULAR((groups,)),
            pltpu.SemaphoreType.REGULAR,
            dma((groups,)), dma((groups,)), dma((groups,)), dma((groups,)),
            dma((3,)), dma((3,)), dma((2,)), dma((2,)), dma((groups,)), dma((groups,)),
            dma, dma, dma((groups,)), dma((groups,)),
            dma((groups,)), dma((groups,)), dma((groups,)), dma((groups,)),
        ],
        compiler_params=pltpu.CompilerParams(collective_id=0, has_side_effects=True, vmem_limit_bytes=VMEM_LIMIT),
        name="poisson_gradient",
    )(
        activity.reshape(area, width), histo_counts, background,
        jnp.swapaxes(blur_values, 2, 3).reshape(total, band, width), jnp.swapaxes(band_start, 0, 1),
    )


def solution(mesh):
    placed = (
        P(("parts", "view"), "slab", None),
        P(("parts", "view"), None, "slab", None),
        P(("parts", "view"), "slab", None),
        P("view", None, None, None),
        P("view", None, None),
    )
    return jax.shard_map(
        per_device,
        mesh=mesh,
        in_specs=placed,
        out_specs=P(("parts", "view"), "slab", None),
        check_vma=False,
    )
```
